256 devices in a mesh: seg: 16 (over z, core), lon: 16 (over y, x).
Axes of the slice: x: 4, y: 4, z: 8, core: 2. Of those that a mesh axis runs over, the one named last changes fastest.
Arguments:
- states: float32 [32, 16, 384, 1024], P('seg', None, 'lon'), may hold values from -20 to 20
- step_counts: int32 [32], replicated, may hold values from 4 to 6, as said below
- land: int32 [384, 1024], P('lon'), may hold values 0 or 1
- east_flow: float32 [384, 1024], P('lon'), may hold values from -0.15 to 0.15
- vert_mix: float32 [16], replicated, may hold values from 0.03 to 0.12
- coupling: float32 [16, 16], replicated, may hold values from -1.5 to 1.5
- amplitude: float32 [32, 16], replicated, may hold values from -4 to 4
- pattern: float32 [16, 384, 1024], P(None, 'lon'), may hold values from -5 to 5
Outputs:
- scaled: float32 [32, 16, 384, 1024], P('seg', None, 'lon')
- mismatch: float32 [], replicated
The draws below stay inside these ranges and needn't reach their ends.
Inputs may be any that keep to these rules, and one draw needn't show every extreme that they name: `step_counts`: some segment takes 6 steps.
All inputs are finite; a program needn't handle non-finite values. No bound on the sum of `land` on one device may be relied on, other than what follows from the above.
Results may differ from the reference program's by a relative error of at most 0.0075.
Values sent between devices are 32-bit elements; how exact they have to be, the bound alone decides.
A program may use at most 64 MiB of HBM per device.

```python
import math
import jax
import jax.numpy as jnp
from jax import lax

TRACERS = 16
STEPS = 6
DEPTH = 16
COLS = 1024
SEGS = 32
NLON = 384


def draw_states(key, part):
    first, second = jax.random.split(jax.random.fold_in(key, 11))
    shape = (SEGS, TRACERS, NLON, COLS)
    place = jnp.arange(NLON, dtype=jnp.float32) / max(NLON - 1, 1)
    rising = jnp.exp(math.log(3.0) * place)[None, None, :, None]
    order = jnp.arange(SEGS, dtype=jnp.float32) / max(SEGS - 1, 1)
    rough = jnp.exp(jax.random.uniform(second, shape, jnp.float32, -0.35, 0.35))
    yearly = jnp.exp(math.log(3.0) * (order - 0.5))[:, None, None, None]
    base = jax.random.truncated_normal(first, -2.5, 2.5, shape, jnp.float32)
    return (base * rough * rising * yearly).astype(jnp.float32)


def draw_step_counts(key, part):
    first, second = jax.random.split(jax.random.fold_in(key, 23))
    counts = jax.random.randint(first, (SEGS,), STEPS - 2, STEPS + 1)
    chosen = jax.random.randint(second, (), 0, SEGS)
    return jnp.where(jnp.arange(SEGS) == chosen, STEPS, counts).astype(jnp.int32)


def set_ends(array, rng, low, high):
    extent = array.shape
    spot = [jax.random.randint(jax.random.fold_in(rng, axis), (), 0, extent[axis]) for axis in range(len(extent))]
    array = array.at[tuple(spot)].set(low)
    longest = extent.index(max(extent))
    spot[longest] = (spot[longest] + 1) % extent[longest]
    return array.at[tuple(spot)].set(high)


def level_of(own_key, dims, cuts, least, top_value):
    loudness = 1.0
    for dim, blocks in cuts:
        draws = jax.random.uniform(jax.random.fold_in(jax.random.fold_in(own_key, 6), dim), (blocks,), jnp.float32, least / len(cuts), top_value / len(cuts))
        loudness = loudness * jnp.repeat(jnp.exp(draws), dims[dim] // blocks).reshape((-1,) + (1,) * (len(dims) - 1 - dim))
    return loudness


def centred(own_key, extent, deviation, most, pieces=(), kind=jnp.bfloat16):
    values = deviation * jax.random.normal(own_key, extent, jnp.float32)
    if pieces:
        values = values * level_of(own_key, extent, pieces, -0.22, 0.18)
    return jnp.clip(values, -most, most).astype(kind)


def setup_inputs(seed: int = 0) -> dict:
    arg_keys = jax.random.split(jax.random.key(seed), 9)
    states = draw_states(jax.random.fold_in(arg_keys[8], 71), 0)
    step_counts = draw_step_counts(jax.random.fold_in(arg_keys[8], 71), 0)
    land = set_ends((jax.random.randint(arg_keys[2], (NLON, COLS), 0, 10) < 9).astype(jnp.int32), jax.random.fold_in(arg_keys[2], 1), 0, 1)
    east_flow = jnp.clip(jax.random.uniform(arg_keys[3], (NLON, COLS), jnp.float32, -0.15, 0.15) * level_of(arg_keys[3], (NLON, COLS), ((0, 16),), -0.4, 0.0), -0.15, 0.15)
    vert_mix = jnp.clip(jnp.exp(jax.random.uniform(arg_keys[4], (TRACERS,), jnp.float32, math.log(0.03), math.log(0.12))), 0.03, 0.12)
    coupling = centred(arg_keys[5], (TRACERS, TRACERS), 0.3, 1.5, (), jnp.float32)
    amplitude = centred(arg_keys[6], (SEGS, TRACERS), 1.0, 4.0, (), jnp.float32)
    pattern = centred(arg_keys[7], (TRACERS, NLON, COLS), 1.0, 5.0, ((1, 16),), jnp.float32)
    return dict(states=states, step_counts=step_counts, land=land, east_flow=east_flow, vert_mix=vert_mix, coupling=coupling, amplitude=amplitude, pattern=pattern)


MIXING = 0.1
STEP_SIZE = 0.1
EPSILON = 1e-06

def advance(field, east, west, water_here, water_east, water_west, current, current_west, pattern, vert_mix, coupling, forcing_amp, active, depth):
    open_east = water_here * water_east
    open_west = water_west * water_here
    flux_east = open_east * (jnp.maximum(current, 0.0) * field + jnp.minimum(current, 0.0) * east)
    flux_west = open_west * (jnp.maximum(current_west, 0.0) * west + jnp.minimum(current_west, 0.0) * field)
    lon_term = MIXING * (open_east * (east - field) - open_west * (field - west)) - (flux_east - flux_west)
    open_north = water_here[:, :-depth] * water_here[:, depth:]
    grad_north = open_north * (field[:, :, depth:] - field[:, :, :-depth])
    grad_north = jnp.pad(grad_north, ((0, 0), (0, 0), (depth, depth)))
    lat_term = MIXING * (grad_north[:, :, depth:] - grad_north[:, :, :-depth])
    cols = field.shape[2]
    inner = ((jnp.arange(cols - 1) + 1) % depth != 0).astype(jnp.float32)
    open_down = water_here[:, :-1] * water_here[:, 1:] * inner
    grad_down = open_down * (field[:, :, 1:] - field[:, :, :-1])
    grad_down = jnp.pad(grad_down, ((0, 0), (0, 0), (1, 1)))
    dep_term = vert_mix[:, None, None] * (grad_down[:, :, 1:] - grad_down[:, :, :-1])
    source = jnp.einsum('ts,slc->tlc', coupling, jnp.tanh(field), precision=lax.Precision.HIGHEST) + forcing_amp[:, None, None] * pattern
    fresh = water_here * (field + lon_term + lat_term + dep_term + STEP_SIZE * source)
    return jnp.where(active, fresh, field)

def reference(states, step_counts, land, east_flow, vert_mix, coupling, amplitude, pattern):
    water = land.astype(jnp.float32)
    water_east = jnp.roll(water, -1, 0)
    water_west = jnp.roll(water, 1, 0)
    current_west = jnp.roll(east_flow, 1, 0)

    def integrate(items):
        field, count, forcing_amp = items
        for section in range(STEPS):
            east = jnp.roll(field, -1, 1)
            west = jnp.roll(field, 1, 1)
            field = advance(field, east, west, water, water_east, water_west, east_flow, current_west, pattern, vert_mix, coupling, forcing_amp, section < count, DEPTH)
        return field
    ends = lax.map(integrate, (states, step_counts, amplitude))
    before = jnp.roll(ends, 1, axis=0)
    resid = water * (before - states)
    msq = lax.optimization_barrier(jnp.mean(resid * resid, axis=(2, 3)))
    scaled = resid / jnp.sqrt(msq + EPSILON)[:, :, None, None]
    mismatch = jnp.sqrt(jnp.mean(msq))
    return (scaled, mismatch)
```

```python
import functools

import jax
import jax.numpy as jnp
from jax import lax
from jax.experimental import pallas as pl
from jax.experimental.pallas import tpu as pltpu
from jax.sharding import PartitionSpec as P

STEPS = 6
DEPTH = 16
MIXING = 0.1
STEP_SIZE = 0.1
EPSILON = 1e-06

HALF = 3
UNROLL = 4
MESH = pl.DeviceIdType.MESH
F32 = jnp.float32
BF16 = jnp.bfloat16


def split(x):
    high = x.astype(BF16)
    return high, (x - high.astype(F32)).astype(BF16)


def twice(x):
    return jnp.concatenate([x, x], 0)


def column(values, tracers):
    row = lax.broadcasted_iota(jnp.int32, (tracers, 128), 0)
    out = jnp.zeros((tracers, 128), F32)
    for t in range(tracers):
        out = jnp.where(row == t, values(t), out)
    return out


def kernel(
    dims,
    states,
    pattern,
    land,
    flow,
    counts,
    vert_mix,
    amplitude,
    coupling,
    out,
    mismatch,
    fields,
    force,
    diag,
    vert,
    press,
    wx,
    ux,
    east_c,
    west_c,
    lat_c,
    near,
    native,
    native_p,
    native_land,
    native_flow,
    shift,
    red,
    year,
    tot,
    load_sem,
    z_send,
    z_recv,
    h_send,
    h_recv,
    s_send,
    s_recv,
    r_send,
    r_recv,
    y_send,
    y_recv,
):
    nseg, nlon, tracers, rows, cols, total_cells = dims
    blocks = cols // 128
    band = 8 * blocks
    stride = rows // 8 * band
    seg = lax.axis_index("seg")
    lon = lax.axis_index("lon")
    lane = lax.broadcasted_iota(jnp.int32, (tracers, 128), 1)
    lane8 = lax.broadcasted_iota(jnp.int32, (8, 128), 1)
    sub8 = lax.broadcasted_iota(jnp.int32, (8, 128), 0)
    zero = jnp.zeros((tracers, 128), F32)
    W = HALF

    barrier = pltpu.get_barrier_semaphore()
    for p in range(1, nlon):
        pl.semaphore_signal(barrier, inc=1, device_id=(seg, (lon + p) % nlon), device_id_type=MESH)
    for p in range(1, nseg):
        pl.semaphore_signal(barrier, inc=1, device_id=((seg + p) % nseg, lon), device_id_type=MESH)

    loads = [
        pltpu.make_async_copy(land, native_land, load_sem.at[0]),
        pltpu.make_async_copy(flow, native_flow, load_sem.at[1]),
        pltpu.make_async_copy(states.at[0], native.at[0], load_sem.at[2]),
        pltpu.make_async_copy(pattern, native_p, load_sem.at[3]),
        pltpu.make_async_copy(states.at[1], native.at[1], load_sem.at[4]),
    ]
    for copy in loads:
        copy.start()

    i = lax.broadcasted_iota(jnp.int32, (256, 128), 0) % 128
    j = lax.broadcasted_iota(jnp.int32, (256, 128), 1)
    apart = (i - j) * (i - j) == 1
    shift[...] = jnp.where(apart & (i // DEPTH == j // DEPTH), 1.0, 0.0).astype(BF16)
    c3 = coupling[...] * STEP_SIZE
    c_high, c_low = split(c3)
    lane3 = lax.broadcasted_iota(jnp.int32, c3.shape, 1)
    weights = jnp.where(
        (lane3 >= tracers) & (lane3 < 2 * tracers), c_low.astype(F32), c_high.astype(F32)
    ).astype(BF16)

    own = 2 * seg
    prev = (own + 2 * nseg - 1) % (2 * nseg)
    vmix = column(lambda t: vert_mix[t], tracers)
    amp = [column(lambda t, s=s: amplitude[s, t], tracers) for s in (own, prev)]

    loads[0].wait()
    loads[1].wait()
    for r in range(rows):
        start = r // 8 * band + r % 8
        wx[pl.ds((r + W) * blocks, blocks), :] = native_land[
            pl.ds(start, blocks, stride=8), :
        ].astype(F32)
        ux[pl.ds((r + W) * blocks, blocks), :] = native_flow[pl.ds(start, blocks, stride=8), :]

    east = (seg, (lon + 1) % nlon)
    west = (seg, (lon + nlon - 1) % nlon)

    def remote(src, dst, send, recv, device):
        return pltpu.make_async_remote_copy(
            src_ref=src, dst_ref=dst, send_sem=send, recv_sem=recv, device_id=device, device_id_type=MESH
        )

    def halo(ref, width, send, recv, scale=1):
        return [
            remote(
                ref.at[pl.ds((W + rows - width) * scale, width * scale)],
                ref.at[pl.ds((W - width) * scale, width * scale)],
                send.at[0],
                recv.at[0],
                east,
            ),
            remote(
                ref.at[pl.ds(W * scale, width * scale)],
                ref.at[pl.ds((W + rows) * scale, width * scale)],
                send.at[1],
                recv.at[1],
                west,
            ),
        ]

    nxt = ((seg + 1) % nseg, lon)
    chunks = (0, rows // 8 - 1) + tuple(range(1, rows // 8 - 1))
    moves = [
        remote(
            states.at[1, :, pl.ds(b * band, band), :],
            near.at[:, pl.ds(b * band, band), :],
            z_send.at[n],
            z_recv.at[n],
            nxt,
        )
        for n, b in enumerate(chunks)
    ]
    static = (
        halo(wx, W, s_send.at[0], s_recv.at[0], blocks)
        + halo(ux, W, s_send.at[1], s_recv.at[1], blocks)
    )
    forcing = halo(press, W - 1, s_send.at[2], s_recv.at[2])
    halos = [
        [halo(fields.at[s, level], W, h_send.at[s, n], h_recv.at[s, n]) for n, level in enumerate((0, HALF))]
        for s in (0, 1)
    ]

    pl.semaphore_wait(barrier, nlon + nseg - 2)
    for copy in moves:
        copy.start()
    for copy in static:
        copy.start()

    def row_w(e, b):
        return twice(wx[pl.ds(e * blocks + b, 8, stride=0), :])

    def native_row(r, b):
        return pl.ds(r // 8 * band + b * 8 + r % 8, tracers, stride=stride)

    own2d = native.at[0].reshape(tracers * stride, 128)
    own2d_1 = native.at[1].reshape(tracers * stride, 128)
    near2d = near.reshape(tracers * stride, 128)
    pat2d = native_p.reshape(tracers * stride, 128)

    def unpack(src2d, dst, first, count, scale=None):
        def body(n, _):
            r = first + n
            for b in range(blocks):
                value = src2d[native_row(r, b), :] * row_w(r + W, b)
                dst[r + W, :, pl.ds(b * 128, 128)] = value if scale is None else value * scale
            return 0

        lax.fori_loop(0, count, body, 0)

    loads[2].wait()
    f0 = fields.at[0, 0]
    unpack(own2d, f0, 0, W)
    unpack(own2d, f0, rows - W, W)
    unpack(own2d, f0, W, rows - 2 * W)
    for copy in halos[0][0]:
        copy.start()
    loads[3].wait()
    unpack(pat2d, press, 0, rows, STEP_SIZE)
    for copy in forcing:
        copy.start()

    def coefficients(first, count):
        def body(n, _):
            e = first + n
            at = lambda ref, k: ref[pl.ds((e + k) * blocks, blocks), :]
            w, w_e, w_w = at(wx, 0), at(wx, 1), at(wx, -1)
            u, u_w = at(ux, 0), at(ux, -1)
            up = pltpu.roll(w, 16, 1)
            down = pltpu.roll(w, 112, 1)
            up_wrap = jnp.where(sub8 == 0, 0.0, pltpu.roll(up, 1, 0))
            down_wrap = jnp.where(sub8 == 7, 0.0, pltpu.roll(down, 7, 0))
            south = jnp.where(lane8 < 16, up_wrap, up)
            north = jnp.where(lane8 >= 112, down_wrap, down)
            level = lane8 % DEPTH
            above = jnp.where(level == 0, 0.0, pltpu.roll(w, 1, 1))
            below = jnp.where(level == DEPTH - 1, 0.0, pltpu.roll(w, 127, 1))
            here = pl.ds(e * blocks, blocks)
            east_c[here, :] = w * (MIXING - jnp.minimum(u, 0.0))
            west_c[here, :] = w * (MIXING + jnp.maximum(u_w, 0.0))
            lat_c[here, :] = w * MIXING
            center = w * (
                1.0
                - MIXING * (w_e + w_w + north + south)
                - w_e * jnp.maximum(u, 0.0)
                + w_w * jnp.minimum(u_w, 0.0)
            )
            faces = w * (above + below)
            tot[0] = center
            tot[1] = faces
            for b in range(blocks):
                a = tot[0, pl.ds(b, 8, stride=0), :]
                f = tot[1, pl.ds(b, 8, stride=0), :]
                s = pl.ds(b * 128, 128)
                diag[e, :, s] = twice(a) - vmix * twice(f)
                vert[e, :, s] = vmix * row_w(e, b)
            return 0

        lax.fori_loop(0, count, body, 0)

    def forces(first, count):
        def body(n, _):
            e = first + n
            for b in range(blocks):
                s = pl.ds(b * 128, 128)
                p = press[e, :, s]
                force[0, e, :, s] = p * amp[0]
                force[1, e, :, s] = p * amp[1]
            return 0

        lax.fori_loop(0, count, body, 0)

    def update(s, level, es, active):
        src = fields.at[s, level]
        dst = fields.at[s, level + 1]
        cells = [[src[e, :, pl.ds(b * 128, 128)] for b in range(blocks)] for e in es]
        parts = [split(c) for row in cells for c in row]
        dep = jnp.dot(
            jnp.concatenate([jnp.concatenate(hl, 1) for hl in parts], 0),
            shift[...],
            preferred_element_type=F32,
        )
        for n, e in enumerate(es):
            row = cells[n]
            mixed = []
            for q in range(blocks // 2):
                high, low = split(jnp.tanh(jnp.concatenate(row[2 * q : 2 * q + 2], 1)))
                mixed.append(
                    jnp.dot(weights, jnp.concatenate([high, high, low], 0), preferred_element_type=F32)
                )
            up = [pltpu.roll(c, 16, 1) for c in row]
            down = [pltpu.roll(c, 112, 1) for c in row]
            for b in range(blocks):
                at = pl.ds(b * 128, 128)
                spread = pl.ds(e * blocks + b, 8, stride=0)
                south = jnp.where(lane < 16, up[b - 1] if b else zero, up[b])
                north = jnp.where(lane >= 112, down[b + 1] if b < blocks - 1 else zero, down[b])
                first = (n * blocks + b) * tracers
                fresh = diag[e, :, at] * row[b]
                fresh = fresh + twice(east_c[spread, :]) * src[e + 1, :, at]
                fresh = fresh + twice(west_c[spread, :]) * src[e - 1, :, at]
                fresh = fresh + twice(lat_c[spread, :]) * (south + north)
                fresh = fresh + vert[e, :, at] * dep[first : first + tracers]
                fresh = fresh + force[s, e, :, at]
                fresh = fresh + mixed[b // 2][:, b % 2 * 128 : b % 2 * 128 + 128]
                dst[e, :, at] = jnp.where(active, fresh, row[b])

    def alive(s, level):
        return jnp.full((tracers, 128), counts[own if s == 0 else prev], jnp.int32) > level

    def interior(s, base):
        def level_body(k, _):
            active = alive(s, base + k)
            groups = (rows - 2 - 2 * k + UNROLL - 1) // UNROLL
            reach = rows - 2 - 2 * k - UNROLL

            def body(g, _):
                first = W + 1 + k + g * reach // (groups - 1)
                update(s, base + k, [first + n for n in range(UNROLL)], active)
                return 0

            lax.fori_loop(0, groups, body, 0)
            return 0

        lax.fori_loop(0, HALF, level_body, 0)

    def edges(s, base):
        def level_body(k, _):
            left = W - 2 + k
            right = W + rows - 1 - k
            es = [left + n for n in range(3)] + [right + n for n in range(3)]
            update(s, base + k, es, alive(s, base + k))
            return 0

        lax.fori_loop(0, HALF, level_body, 0)

    def residual(s, body_value):
        def body(r, acc):
            for b in range(blocks):
                at = pl.ds(b * 128, 128)
                value = fields[s, STEPS, r + W, :, at] - body_value(r, b)
                fields[s, STEPS, r + W, :, at] = value
                acc = acc + value * value
            return acc

        return lax.fori_loop(0, rows, body, zero)

    def publish(s, value):
        red[s, lon] = value
        sends = []
        for p in range(1, nlon):
            peer = (lon + p) % nlon
            copy = remote(red.at[s, lon], red.at[s, lon], r_send.at[s, p], r_recv.at[s, p], (seg, peer))
            copy.start()
            sends.append(copy)
        return sends

    def finish(s, sends, slot):
        for copy in sends:
            copy.wait()
        square = red[s, 0]
        for p in range(1, nlon):
            square = square + red[s, p]
        mean = jnp.broadcast_to(jnp.sum(square, axis=1, keepdims=True), (tracers, 128)) / total_cells
        root = jnp.sqrt(mean + EPSILON)
        return mean, root

    def scale(s, root, slot):
        inverse = 1.0 / root
        target = out.at[slot].reshape(tracers * stride, 128)

        def body(r, _):
            for b in range(blocks):
                target[native_row(r, b), :] = fields[s, STEPS, r + W, :, pl.ds(b * 128, 128)] * inverse
            return 0

        lax.fori_loop(0, rows, body, 0)

    coefficients(W + 1, rows - 2)
    forces(W + 1, rows - 2)
    interior(0, 0)
    for copy in static:
        copy.wait()
    for copy in forcing:
        copy.wait()
    coefficients(1, W)
    coefficients(W + rows - 1, W)
    forces(1, W)
    forces(W + rows - 1, W)
    for copy in halos[0][0]:
        copy.wait()
    edges(0, 0)
    for copy in halos[0][1]:
        copy.start()

    g0 = fields.at[1, 0]
    moves[0].wait()
    unpack(near2d, g0, 0, 8)
    halos[1][0][1].start()

    interior(0, HALF)
    moves[1].wait()
    unpack(near2d, g0, rows - 8, 8)
    halos[1][0][0].start()
    for copy in halos[0][1]:
        copy.wait()
    edges(0, HALF)
    loads[4].wait()
    sends_own = publish(0, residual(0, lambda r, b: own2d_1[native_row(r, b), :] * row_w(r + W, b)))

    for copy in moves[2:]:
        copy.wait()
    unpack(near2d, g0, 8, rows - 16)
    interior(1, 0)
    for copy in halos[1][0]:
        copy.wait()
    edges(1, 0)
    for copy in halos[1][1]:
        copy.start()
    interior(1, HALF)
    for copy in halos[1][1]:
        copy.wait()
    edges(1, HALF)
    sends_prev = publish(1, residual(1, lambda r, b: fields[0, 0, r + W, :, pl.ds(b * 128, 128)]))
    mean_own, root_own = finish(0, sends_own, 1)
    scale(0, root_own, 1)
    mean_prev, root_prev = finish(1, sends_prev, 0)

    local = mean_own + mean_prev
    local = jnp.sum(local, axis=0, keepdims=True)
    year[seg] = jnp.broadcast_to(local, (8, 128))
    sends = []
    for p in range(1, nseg):
        peer = (seg + p) % nseg
        copy = remote(year.at[seg], year.at[seg], y_send.at[p], y_recv.at[p], (peer, lon))
        copy.start()
        sends.append(copy)
    scale(1, root_prev, 0)
    for copy in sends:
        copy.wait()
    whole = year[0]
    for p in range(1, nseg):
        whole = whole + year[p]
    mismatch[0, 0] = jnp.sqrt(whole / (2 * nseg * tracers))[0, 0]


def shards(mesh, states, step_counts, land, east_flow, vert_mix, coupling, amplitude, pattern):
    nseg, nlon = mesh.shape["seg"], mesh.shape["lon"]
    per, tracers, rows, cols = states.shape
    blocks = cols // 128
    stride = rows * blocks

    def tiles(x):
        lead = x.shape[:-2]
        x = x.reshape(lead + (rows // 8, 8, blocks, 128))
        return jnp.swapaxes(x, -2, -3).reshape(lead + (stride, 128))

    ext = rows + 2 * HALF
    any_spec = pl.BlockSpec(memory_space=pl.ANY)
    smem = pl.BlockSpec(memory_space=pltpu.SMEM)
    vmem = pl.BlockSpec(memory_space=pltpu.VMEM)
    dma = pltpu.SemaphoreType.DMA
    dims = (nseg, nlon, tracers, rows, cols, rows * nlon * cols)
    out, mismatch = pl.pallas_call(
        functools.partial(kernel, dims),
        out_shape=(
            jax.ShapeDtypeStruct((per, tracers, stride, 128), F32),
            jax.ShapeDtypeStruct((1, 1), F32),
        ),
        in_specs=[any_spec] * 4 + [smem] * 3 + [vmem],
        out_specs=(vmem, smem),
        scratch_shapes=[
            pltpu.VMEM((2, STEPS + 1, ext, tracers, cols), F32),
            pltpu.VMEM((2, ext, tracers, cols), F32),
            pltpu.VMEM((ext, tracers, cols), F32),
            pltpu.VMEM((ext, tracers, cols), F32),
            pltpu.VMEM((ext, tracers, cols), F32),
            pltpu.VMEM((ext * blocks, 128), F32),
            pltpu.VMEM((ext * blocks, 128), F32),
            pltpu.VMEM((ext * blocks, 128), F32),
            pltpu.VMEM((ext * blocks, 128), F32),
            pltpu.VMEM((ext * blocks, 128), F32),
            pltpu.VMEM((tracers, stride, 128), F32),
            pltpu.VMEM((2, tracers, stride, 128), F32),
            pltpu.VMEM((tracers, stride, 128), F32),
            pltpu.VMEM((stride, 128), jnp.int32),
            pltpu.VMEM((stride, 128), F32),
            pltpu.VMEM((256, 128), BF16),
            pltpu.VMEM((2, nlon, tracers, 128), F32),
            pltpu.VMEM((nseg, 8, 128), F32),
            pltpu.VMEM((2, 8, 128), F32),
            dma((5,)),
            dma((rows // 8,)),
            dma((rows // 8,)),
            dma((2, 2, 2)),
            dma((2, 2, 2)),
            dma((3, 2)),
            dma((3, 2)),
            dma((2, nlon)),
            dma((2, nlon)),
            dma((nseg,)),
            dma((nseg,)),
        ],
        compiler_params=pltpu.CompilerParams(
            collective_id=0, has_side_effects=True, vmem_limit_bytes=60 * 1024 * 1024
        ),
    )(
        tiles(states),
        tiles(pattern),
        tiles(land),
        tiles(east_flow),
        step_counts,
        vert_mix,
        amplitude,
        jnp.concatenate([coupling] * 3, axis=1),
    )
    out = out.reshape(per, tracers, rows // 8, blocks, 8, 128)
    out = jnp.swapaxes(out, -2, -3).reshape(states.shape)
    return out, mismatch.reshape(())


def solution(mesh):
    in_specs = (
        P("seg", None, "lon", None),
        P(),
        P("lon", None),
        P("lon", None),
        P(),
        P(),
        P(),
        P(None, "lon", None),
    )
    out_specs = (P("seg", None, "lon", None), P())
    return jax.shard_map(
        functools.partial(shards, mesh), mesh=mesh, in_specs=in_specs, out_specs=out_specs, check_vma=False
    )
```

```python
import functools

import jax
import jax.numpy as jnp
from jax import lax
from jax.experimental import pallas as pl
from jax.experimental.pallas import tpu as pltpu
from jax.sharding import PartitionSpec as P

STEPS = 6
DEPTH = 16
MIXING = 0.1
STEP_SIZE = 0.1
EPSILON = 1e-06

HALF = 3
UNROLL = 4
LEAST_STEPS = 4
MESH = pl.DeviceIdType.MESH
F32 = jnp.float32
BF16 = jnp.bfloat16


def split(x):
    high = x.astype(BF16)
    return high, (x - high.astype(F32)).astype(BF16)


def twice(x):
    return jnp.concatenate([x, x], 0)


def column(values, tracers):
    row = lax.broadcasted_iota(jnp.int32, (tracers, 128), 0)
    out = jnp.zeros((tracers, 128), F32)
    for t in range(tracers):
        out = jnp.where(row == t, values(t), out)
    return out


def kernel(
    dims,
    states,
    pattern,
    land,
    flow,
    counts,
    vert_mix,
    amplitude,
    coupling,
    out,
    mismatch,
    f_own_0,
    f_own_3,
    f_own_6,
    f_prev_0,
    f_prev_3,
    f_prev_6,
    f_1,
    f_2,
    f_4,
    f_5,
    diag,
    vert,
    press,
    parts,
    wx,
    ux,
    east_c,
    west_c,
    lat_c,
    near,
    native,
    native_p,
    native_land,
    native_flow,
    shift,
    red,
    year,
    tot,
    lhs,
    load_sem,
    store_sem,
    z_send,
    z_recv,
    h_send,
    h_recv,
    s_send,
    s_recv,
    r_send,
    r_recv,
    y_send,
    y_recv,
):
    nseg, nlon, tracers, rows, cols, total_cells = dims
    blocks = cols // 128
    band = 8 * blocks
    native_rows = rows // 8 * band
    stride = native_rows + 8
    fields = ((f_own_0, f_1, f_2, f_own_3, f_4, f_5, f_own_6), (f_prev_0, f_1, f_2, f_prev_3, f_4, f_5, f_prev_6))
    seg = lax.axis_index("seg")
    lon = lax.axis_index("lon")
    lane = lax.broadcasted_iota(jnp.int32, (tracers, 128), 1)
    lane8 = lax.broadcasted_iota(jnp.int32, (8, 128), 1)
    sub8 = lax.broadcasted_iota(jnp.int32, (8, 128), 0)
    zero = jnp.zeros((tracers, 128), F32)
    W = HALF

    barrier = pltpu.get_barrier_semaphore()
    for p in range(1, nlon):
        pl.semaphore_signal(barrier, inc=1, device_id=(seg, (lon + p) % nlon), device_id_type=MESH)
    for p in range(1, nseg):
        pl.semaphore_signal(barrier, inc=1, device_id=((seg + p) % nseg, lon), device_id_type=MESH)

    loads = [
        pltpu.make_async_copy(land, native_land, load_sem.at[0]),
        pltpu.make_async_copy(flow, native_flow, load_sem.at[1]),
        pltpu.make_async_copy(states.at[0], native.at[0, :, pl.ds(0, native_rows)], load_sem.at[2]),
        pltpu.make_async_copy(pattern, native_p.at[:, pl.ds(0, native_rows)], load_sem.at[3]),
        pltpu.make_async_copy(states.at[1], native.at[1, :, pl.ds(0, native_rows)], load_sem.at[4]),
    ]
    for copy in loads:
        copy.start()

    i = lax.broadcasted_iota(jnp.int32, (256, 128), 0) % 128
    j = lax.broadcasted_iota(jnp.int32, (256, 128), 1)
    apart = (i - j) * (i - j) == 1
    shift[...] = jnp.where(apart & (i // DEPTH == j // DEPTH), 1.0, 0.0).astype(BF16)
    own = 2 * seg
    prev = (own + 2 * nseg - 1) % (2 * nseg)
    vmix = column(lambda t: vert_mix[t], tracers)

    lhs[...] = jnp.zeros((tracers, 128), F32)
    lhs[:, 0:tracers] = coupling[...] * STEP_SIZE
    c_high, c_low = (x.astype(F32) for x in split(lhs[...]))
    c_low = pltpu.roll(c_low, tracers, 1)
    place = lane // tracers
    on_diagonal = lane % tracers == lax.broadcasted_iota(jnp.int32, (tracers, 128), 0)
    mixers = []
    for s in (own, prev):
        a_high, a_low = (
            jnp.where(on_diagonal, x.astype(F32), 0.0)
            for x in split(column(lambda t, s=s: amplitude[t, s], tracers))
        )
        joined = jnp.where(place == 0, c_high, jnp.where(place == 1, c_low, jnp.where(place == 3, a_low, a_high)))
        mixers.append(joined.astype(BF16)[:, : 5 * tracers])

    loads[0].wait()
    loads[1].wait()
    for r in range(rows):
        start = r // 8 * band + r % 8
        wx[pl.ds((r + W) * blocks, blocks), :] = native_land[
            pl.ds(start, blocks, stride=8), :
        ].astype(F32)
        ux[pl.ds((r + W) * blocks, blocks), :] = native_flow[pl.ds(start, blocks, stride=8), :]

    east = (seg, (lon + 1) % nlon)
    west = (seg, (lon + nlon - 1) % nlon)

    def remote(src, dst, send, recv, device):
        return pltpu.make_async_remote_copy(
            src_ref=src, dst_ref=dst, send_sem=send, recv_sem=recv, device_id=device, device_id_type=MESH
        )

    def halo(ref, width, send, recv, scale=1):
        return [
            remote(
                ref.at[pl.ds((W + rows - width) * scale, width * scale)],
                ref.at[pl.ds((W - width) * scale, width * scale)],
                send.at[0],
                recv.at[0],
                east,
            ),
            remote(
                ref.at[pl.ds(W * scale, width * scale)],
                ref.at[pl.ds((W + rows) * scale, width * scale)],
                send.at[1],
                recv.at[1],
                west,
            ),
        ]

    nxt = ((seg + 1) % nseg, lon)
    chunks = (0, rows // 8 - 1) + tuple(range(1, rows // 8 - 1))
    moves = [
        remote(
            states.at[1, :, pl.ds(b * band, band), :],
            near.at[:, pl.ds(b * band, band), :],
            z_send.at[n],
            z_recv.at[n],
            nxt,
        )
        for n, b in enumerate(chunks)
    ]
    static = (
        halo(wx, W, s_send.at[0], s_recv.at[0], blocks)
        + halo(ux, W, s_send.at[1], s_recv.at[1], blocks)
    )
    forcing = halo(press, W - 1, s_send.at[2], s_recv.at[2])
    halos = [
        [halo(fields[s][level], W, h_send.at[s, n], h_recv.at[s, n]) for n, level in enumerate((0, HALF))]
        for s in (0, 1)
    ]

    def row_w(e, b):
        return twice(wx[pl.ds(e * blocks + b, 8, stride=0), :])

    def native_row(r, b):
        return pl.ds(r // 8 * band + b * 8 + r % 8, tracers, stride=stride)

    own2d = native.at[0].reshape(tracers * stride, 128)
    own2d_1 = native.at[1].reshape(tracers * stride, 128)
    near2d = near.reshape(tracers * stride, 128)
    pat2d = native_p.reshape(tracers * stride, 128)

    def unpack(src2d, dst, first, count, scale=None):
        def body(n, _):
            r = first + n
            for b in range(blocks):
                value = src2d[native_row(r, b), :] * row_w(r + W, b)
                dst[r + W, :, pl.ds(b * 128, 128)] = value if scale is None else value * scale
            return 0

        lax.fori_loop(0, count, body, 0)

    loads[2].wait()
    f0 = fields[0][0]
    unpack(own2d, f0, 0, W)
    unpack(own2d, f0, rows - W, W)
    unpack(own2d, f0, W, rows - 2 * W)
    loads[3].wait()
    unpack(pat2d, press, 0, rows, STEP_SIZE)
    pl.semaphore_wait(barrier, nlon + nseg - 2)
    for copy in static + halos[0][0] + forcing + moves:
        copy.start()

    def coefficients(first, count):
        def body(n, _):
            e = first + n
            at = lambda ref, k: ref[pl.ds((e + k) * blocks, blocks), :]
            w, w_e, w_w = at(wx, 0), at(wx, 1), at(wx, -1)
            u, u_w = at(ux, 0), at(ux, -1)
            up = pltpu.roll(w, 16, 1)
            down = pltpu.roll(w, 112, 1)
            up_wrap = jnp.where(sub8 == 0, 0.0, pltpu.roll(up, 1, 0))
            down_wrap = jnp.where(sub8 == 7, 0.0, pltpu.roll(down, 7, 0))
            south = jnp.where(lane8 < 16, up_wrap, up)
            north = jnp.where(lane8 >= 112, down_wrap, down)
            level = lane8 % DEPTH
            above = jnp.where(level == 0, 0.0, pltpu.roll(w, 1, 1))
            below = jnp.where(level == DEPTH - 1, 0.0, pltpu.roll(w, 127, 1))
            here = pl.ds(e * blocks, blocks)
            east_c[here, :] = w * (MIXING - jnp.minimum(u, 0.0))
            west_c[here, :] = w * (MIXING + jnp.maximum(u_w, 0.0))
            lat_c[here, :] = w * MIXING
            center = w * (
                1.0
                - MIXING * (w_e + w_w + north + south)
                - w_e * jnp.maximum(u, 0.0)
                + w_w * jnp.minimum(u_w, 0.0)
            )
            faces = w * (above + below)
            tot[0] = center
            tot[1] = faces
            for b in range(blocks):
                a = tot[0, pl.ds(b, 8, stride=0), :]
                f = tot[1, pl.ds(b, 8, stride=0), :]
                s = pl.ds(b * 128, 128)
                diag[e, :, s] = twice(a) - vmix * twice(f)
                vert[e, :, s] = vmix * row_w(e, b)
            return 0

        lax.fori_loop(0, count, body, 0)

    def forces(first, count):
        def body(n, _):
            e = first + n
            for b in range(blocks):
                at = pl.ds(b * 128, 128)
                high, low = split(press[e, :, at])
                parts[e, 0:tracers, at] = high
                parts[e, tracers : 2 * tracers, at] = low
            return 0

        lax.fori_loop(0, count, body, 0)

    def mix(src, s, es):
        cells = [[src[e, :, pl.ds(b * 128, 128)] for b in range(blocks)] for e in es]
        pairs = [split(c) for row in cells for c in row]
        dep = jnp.dot(
            jnp.concatenate([jnp.concatenate(hl, 1) for hl in pairs], 0),
            shift[...],
            preferred_element_type=F32,
        )
        results = []
        for n, e in enumerate(es):
            row = cells[n]
            mixed = []
            for q in range(blocks // 2):
                at = pl.ds(q * 256, 256)
                t = jnp.tanh(jnp.concatenate(row[2 * q : 2 * q + 2], 1)).astype(BF16)
                high, low = parts[e, 0:tracers, at], parts[e, tracers : 2 * tracers, at]
                mixed.append(
                    jnp.dot(
                        mixers[s], jnp.concatenate([t, t, high, high, low], 0), preferred_element_type=F32
                    )
                )
            first = n * blocks * tracers
            results.append(
                (row, [dep[first + b * tracers : first + (b + 1) * tracers] for b in range(blocks)], mixed)
            )
        return results

    def combine(src, dst, e, result, active):
        row, dep, mixed = result
        up = [pltpu.roll(c, 16, 1) for c in row]
        down = [pltpu.roll(c, 112, 1) for c in row]
        for b in range(blocks):
            at = pl.ds(b * 128, 128)
            spread = pl.ds(e * blocks + b, 8, stride=0)
            south = jnp.where(lane < 16, up[b - 1] if b else zero, up[b])
            north = jnp.where(lane >= 112, down[b + 1] if b < blocks - 1 else zero, down[b])
            fresh = diag[e, :, at] * row[b]
            fresh = fresh + twice(east_c[spread, :]) * src[e + 1, :, at]
            fresh = fresh + twice(west_c[spread, :]) * src[e - 1, :, at]
            fresh = fresh + twice(lat_c[spread, :]) * (south + north)
            fresh = fresh + vert[e, :, at] * dep[b]
            fresh = fresh + mixed[b // 2][:, b % 2 * 128 : b % 2 * 128 + 128]
            dst[e, :, at] = fresh if active is None else jnp.where(active, fresh, row[b])

    def update(s, level, es):
        src, dst = fields[s][level], fields[s][level + 1]
        active = alive(s, level) if level >= LEAST_STEPS else None
        waiting = None
        for i in range(0, len(es), UNROLL):
            group = es[i : i + UNROLL]
            results = mix(src, s, group)
            if waiting is not None:
                for e, result in zip(*waiting):
                    combine(src, dst, e, result, active)
            waiting = (group, results)
        for e, result in zip(*waiting):
            combine(src, dst, e, result, active)

    def span(s, level, first, count):
        def body(g, _):
            update(s, level, [first + g * (count // 2) + n for n in range(count // 2)])
            return 0

        lax.fori_loop(0, 2, body, 0)

    def alive(s, level):
        return jnp.full((tracers, 128), counts[own if s == 0 else prev], jnp.int32) > level

    def interior(s, base):
        for k in range(HALF):
            span(s, base + k, W + 1 + k, rows - 2 - 2 * k)

    def edges(s, base):
        for k in range(HALF):
            left, right = W - 2 + k, W + rows - 1 - k
            update(s, base + k, [left + n for n in range(3)] + [right + n for n in range(3)])

    def whole(s, base):
        for k in range(HALF):
            span(s, base + k, 1 + k, rows + 4 - 2 * k)

    def residual(s, body_value):
        def body(r, acc):
            for b in range(blocks):
                at = pl.ds(b * 128, 128)
                value = fields[s][STEPS][r + W, :, at] - body_value(r, b)
                fields[s][STEPS][r + W, :, at] = value
                acc = acc + value * value
            return acc

        return lax.fori_loop(0, rows, body, zero)

    def publish(s, value):
        red[s, lon] = value
        sends = []
        for p in range(1, nlon):
            peer = (lon + p) % nlon
            copy = remote(red.at[s, lon], red.at[s, lon], r_send.at[s, p], r_recv.at[s, p], (seg, peer))
            copy.start()
            sends.append(copy)
        return sends

    def finish(s, sends):
        for copy in sends:
            copy.wait()
        square = red[s, 0]
        for p in range(1, nlon):
            square = square + red[s, p]
        mean = jnp.broadcast_to(jnp.sum(square, axis=1, keepdims=True), (tracers, 128)) / total_cells
        root = jnp.sqrt(mean + EPSILON)
        return mean, root

    def scale(s, root, slot):
        inverse = 1.0 / root
        buffer = native.at[0] if s == 0 else near
        target = buffer.reshape(tracers * stride, 128)

        def body(r, _):
            for b in range(blocks):
                target[native_row(r, b), :] = fields[s][STEPS][r + W, :, pl.ds(b * 128, 128)] * inverse
            return 0

        lax.fori_loop(0, rows, body, 0)
        copy = pltpu.make_async_copy(buffer.at[:, pl.ds(0, native_rows)], out.at[slot], store_sem.at[s])
        copy.start()
        return copy

    coefficients(W + 1, rows - 2)
    forces(W + 1, rows - 2)
    interior(0, 0)
    for copy in static:
        copy.wait()
    for copy in forcing:
        copy.wait()
    coefficients(1, W)
    coefficients(W + rows - 1, W)
    forces(1, W)
    forces(W + rows - 1, W)
    for copy in halos[0][0]:
        copy.wait()
    edges(0, 0)
    for copy in halos[0][1]:
        copy.start()

    g0 = fields[1][0]
    moves[0].wait()
    unpack(near2d, g0, 0, 8)
    halos[1][0][1].start()

    interior(0, HALF)
    moves[1].wait()
    unpack(near2d, g0, rows - 8, 8)
    halos[1][0][0].start()
    for copy in halos[0][1]:
        copy.wait()
    edges(0, HALF)
    loads[4].wait()
    sends_own = publish(0, residual(0, lambda r, b: own2d_1[native_row(r, b), :] * row_w(r + W, b)))

    for copy in moves[2:]:
        copy.wait()
    unpack(near2d, g0, 8, rows - 16)
    for copy in halos[1][0]:
        copy.wait()
    whole(1, 0)
    for copy in halos[1][1]:
        copy.start()
    interior(1, HALF)
    for copy in halos[1][1]:
        copy.wait()
    edges(1, HALF)
    sends_prev = publish(1, residual(1, lambda r, b: fields[0][0][r + W, :, pl.ds(b * 128, 128)]))
    mean_own, root_own = finish(0, sends_own)
    stored = [scale(0, root_own, 1)]
    mean_prev, root_prev = finish(1, sends_prev)

    local = mean_own + mean_prev
    local = jnp.sum(local, axis=0, keepdims=True)
    year[seg] = jnp.broadcast_to(local, (8, 128))
    sends = []
    for p in range(1, nseg):
        peer = (seg + p) % nseg
        copy = remote(year.at[seg], year.at[seg], y_send.at[p], y_recv.at[p], (peer, lon))
        copy.start()
        sends.append(copy)
    stored.append(scale(1, root_prev, 0))
    for copy in sends:
        copy.wait()
    total = year[0]
    for p in range(1, nseg):
        total = total + year[p]
    for copy in stored:
        copy.wait()
    mismatch[0, 0] = jnp.sqrt(total / (2 * nseg * tracers))[0, 0]


def shards(mesh, states, step_counts, land, east_flow, vert_mix, coupling, amplitude, pattern):
    nseg, nlon = mesh.shape["seg"], mesh.shape["lon"]
    per, tracers, rows, cols = states.shape
    blocks = cols // 128
    stride = rows * blocks

    def tiles(x):
        lead = x.shape[:-2]
        x = x.reshape(lead + (rows // 8, 8, blocks, 128))
        return jnp.swapaxes(x, -2, -3).reshape(lead + (stride, 128))

    ext = rows + 2 * HALF
    any_spec = pl.BlockSpec(memory_space=pl.ANY)
    smem = pl.BlockSpec(memory_space=pltpu.SMEM)
    vmem = pl.BlockSpec(memory_space=pltpu.VMEM)
    dma = pltpu.SemaphoreType.DMA
    dims = (nseg, nlon, tracers, rows, cols, rows * nlon * cols)
    out, mismatch = pl.pallas_call(
        functools.partial(kernel, dims),
        out_shape=(
            jax.ShapeDtypeStruct((per, tracers, stride, 128), F32),
            jax.ShapeDtypeStruct((1, 1), F32),
        ),
        in_specs=[any_spec] * 4 + [smem] * 3 + [vmem],
        out_specs=(any_spec, smem),
        scratch_shapes=[
            *[pltpu.VMEM((ext, tracers, cols), F32)] * 10,
            *[pltpu.VMEM((ext, tracers, cols), F32)] * 3,
            pltpu.VMEM((ext, 2 * tracers, cols), BF16),
            pltpu.VMEM((ext * blocks, 128), F32),
            pltpu.VMEM((ext * blocks, 128), F32),
            pltpu.VMEM((ext * blocks, 128), F32),
            pltpu.VMEM((ext * blocks, 128), F32),
            pltpu.VMEM((ext * blocks, 128), F32),
            pltpu.VMEM((tracers, stride + 8, 128), F32),
            pltpu.VMEM((2, tracers, stride + 8, 128), F32),
            pltpu.VMEM((tracers, stride + 8, 128), F32),
            pltpu.VMEM((stride, 128), jnp.int32),
            pltpu.VMEM((stride, 128), F32),
            pltpu.VMEM((256, 128), BF16),
            pltpu.VMEM((2, nlon, tracers, 128), F32),
            pltpu.VMEM((nseg, 8, 128), F32),
            pltpu.VMEM((2, 8, 128), F32),
            pltpu.VMEM((tracers, 128), F32),
            dma((5,)),
            dma((2,)),
            dma((rows // 8,)),
            dma((rows // 8,)),
            dma((2, 2, 2)),
            dma((2, 2, 2)),
            dma((3, 2)),
            dma((3, 2)),
            dma((2, nlon)),
            dma((2, nlon)),
            dma((nseg,)),
            dma((nseg,)),
        ],
        compiler_params=pltpu.CompilerParams(
            collective_id=0, has_side_effects=True, vmem_limit_bytes=44 * 1024 * 1024
        ),
    )(
        tiles(states),
        tiles(pattern),
        tiles(land),
        tiles(east_flow),
        step_counts,
        vert_mix,
        amplitude.T,
        coupling,
    )
    out = out.reshape(per, tracers, rows // 8, blocks, 8, 128)
    out = jnp.swapaxes(out, -2, -3).reshape(states.shape)
    return out, mismatch.reshape(())


def solution(mesh):
    in_specs = (
        P("seg", None, "lon", None),
        P(),
        P("lon", None),
        P("lon", None),
        P(),
        P(),
        P(),
        P(None, "lon", None),
    )
    out_specs = (P("seg", None, "lon", None), P())
    return jax.shard_map(
        functools.partial(shards, mesh), mesh=mesh, in_specs=in_specs, out_specs=out_specs, check_vma=False
    )
```

```python
import functools

import jax
import jax.numpy as jnp
from jax import lax
from jax.experimental import pallas as pl
from jax.experimental.pallas import tpu as pltpu
from jax.sharding import PartitionSpec as P

STEPS = 6
DEPTH = 16
MIXING = 0.1
STEP_SIZE = 0.1
EPSILON = 1e-06

HALF = 3
UNROLL = 4
LEAST_STEPS = 4
MESH = pl.DeviceIdType.MESH
F32 = jnp.float32
BF16 = jnp.bfloat16


def split(x):
    high = x.astype(BF16)
    return high, (x - high.astype(F32)).astype(BF16)


def twice(x):
    return jnp.concatenate([x, x], 0)


def column(values, tracers):
    row = lax.broadcasted_iota(jnp.int32, (tracers, 128), 0)
    out = jnp.zeros((tracers, 128), F32)
    for t in range(tracers):
        out = jnp.where(row == t, values(t), out)
    return out


def kernel(
    dims,
    states,
    pattern,
    land,
    flow,
    counts,
    vert_mix,
    amplitude,
    coupling,
    out,
    mismatch,
    f_own_0,
    f_own_3,
    f_own_6,
    f_prev_0,
    f_prev_3,
    f_prev_6,
    f_1,
    f_2,
    f_4,
    f_5,
    diag,
    vert,
    press,
    parts,
    wx,
    ux,
    east_c,
    west_c,
    lat_c,
    near,
    native,
    native_p,
    native_land,
    native_flow,
    shift,
    red,
    year,
    tot,
    lhs,
    load_sem,
    store_sem,
    z_send,
    z_recv,
    h_send,
    h_recv,
    s_send,
    s_recv,
    r_send,
    r_recv,
    y_send,
    y_recv,
):
    nseg, nlon, tracers, rows, cols, total_cells = dims
    blocks = cols // 128
    band = 8 * blocks
    native_rows = rows // 8 * band
    stride = native_rows + 8
    fields = ((f_own_0, f_1, f_2, f_own_3, f_4, f_5, f_own_6), (f_prev_0, f_1, f_2, f_prev_3, f_4, f_5, f_prev_6))
    seg = lax.axis_index("seg")
    lon = lax.axis_index("lon")
    lane = lax.broadcasted_iota(jnp.int32, (tracers, 128), 1)
    lane8 = lax.broadcasted_iota(jnp.int32, (8, 128), 1)
    sub8 = lax.broadcasted_iota(jnp.int32, (8, 128), 0)
    zero = jnp.zeros((tracers, 128), F32)
    W = HALF

    barrier = pltpu.get_barrier_semaphore()
    for p in range(1, nlon):
        pl.semaphore_signal(barrier, inc=1, device_id=(seg, (lon + p) % nlon), device_id_type=MESH)
    for p in range(1, nseg):
        pl.semaphore_signal(barrier, inc=1, device_id=((seg + p) % nseg, lon), device_id_type=MESH)

    loads = [
        pltpu.make_async_copy(land, native_land, load_sem.at[0]),
        pltpu.make_async_copy(flow, native_flow, load_sem.at[1]),
        pltpu.make_async_copy(states.at[0], native.at[0, :, pl.ds(0, native_rows)], load_sem.at[2]),
        pltpu.make_async_copy(pattern, native_p.at[:, pl.ds(0, native_rows)], load_sem.at[3]),
        pltpu.make_async_copy(states.at[1], native.at[1, :, pl.ds(0, native_rows)], load_sem.at[4]),
    ]
    for copy in loads:
        copy.start()

    i = lax.broadcasted_iota(jnp.int32, (256, 128), 0) % 128
    j = lax.broadcasted_iota(jnp.int32, (256, 128), 1)
    apart = (i - j) * (i - j) == 1
    shift[...] = jnp.where(apart & (i // DEPTH == j // DEPTH), 1.0, 0.0).astype(BF16)
    own = 2 * seg
    prev = (own + 2 * nseg - 1) % (2 * nseg)
    vmix = column(lambda t: vert_mix[t], tracers)

    lhs[...] = jnp.zeros((tracers, 128), F32)
    lhs[:, 0:tracers] = coupling[...] * STEP_SIZE
    c_high, c_low = (x.astype(F32) for x in split(lhs[...]))
    c_low = pltpu.roll(c_low, tracers, 1)
    place = lane // tracers
    on_diagonal = lane % tracers == lax.broadcasted_iota(jnp.int32, (tracers, 128), 0)
    first_diagonal = on_diagonal & (place == 0)
    mixers = []
    for s in (own, prev):
        a_high, a_low = (
            jnp.where(on_diagonal, x.astype(F32), 0.0)
            for x in split(column(lambda t, s=s: amplitude[t, s], tracers))
        )
        joined = jnp.where(place == 0, c_high, jnp.where(place == 1, c_low, jnp.where(place == 3, a_low, a_high)))
        mixers.append(joined.astype(BF16)[:, : 5 * tracers])

    loads[0].wait()
    loads[1].wait()
    for r in range(rows):
        start = r // 8 * band + r % 8
        wx[pl.ds((r + W) * blocks, blocks), :] = native_land[
            pl.ds(start, blocks, stride=8), :
        ].astype(F32)
        ux[pl.ds((r + W) * blocks, blocks), :] = native_flow[pl.ds(start, blocks, stride=8), :]

    east = (seg, (lon + 1) % nlon)
    west = (seg, (lon + nlon - 1) % nlon)

    def remote(src, dst, send, recv, device):
        return pltpu.make_async_remote_copy(
            src_ref=src, dst_ref=dst, send_sem=send, recv_sem=recv, device_id=device, device_id_type=MESH
        )

    def halo(ref, width, send, recv, scale=1):
        return [
            remote(
                ref.at[pl.ds((W + rows - width) * scale, width * scale)],
                ref.at[pl.ds((W - width) * scale, width * scale)],
                send.at[0],
                recv.at[0],
                east,
            ),
            remote(
                ref.at[pl.ds(W * scale, width * scale)],
                ref.at[pl.ds((W + rows) * scale, width * scale)],
                send.at[1],
                recv.at[1],
                west,
            ),
        ]

    nxt = ((seg + 1) % nseg, lon)
    chunks = (0, rows // 8 - 1) + tuple(range(1, rows // 8 - 1))
    moves = [
        remote(
            states.at[1, :, pl.ds(b * band, band), :],
            near.at[:, pl.ds(b * band, band), :],
            z_send.at[n],
            z_recv.at[n],
            nxt,
        )
        for n, b in enumerate(chunks)
    ]
    static = (
        halo(wx, W, s_send.at[0], s_recv.at[0], blocks)
        + halo(ux, W, s_send.at[1], s_recv.at[1], blocks)
    )
    forcing = halo(press, W - 1, s_send.at[2], s_recv.at[2])
    halos = [
        [halo(fields[s][level], W, h_send.at[s, n], h_recv.at[s, n]) for n, level in enumerate((0, HALF))]
        for s in (0, 1)
    ]

    def row_w(e, b):
        return twice(wx[pl.ds(e * blocks + b, 8, stride=0), :])

    def native_row(r, b):
        return pl.ds(r // 8 * band + b * 8 + r % 8, tracers, stride=stride)

    own2d = native.at[0].reshape(tracers * stride, 128)
    own2d_1 = native.at[1].reshape(tracers * stride, 128)
    near2d = near.reshape(tracers * stride, 128)
    pat2d = native_p.reshape(tracers * stride, 128)

    def unpack(src2d, dst, first, count, scale=None):
        def body(n, _):
            r = first + n
            for b in range(blocks):
                value = src2d[native_row(r, b), :] * row_w(r + W, b)
                dst[r + W, :, pl.ds(b * 128, 128)] = value if scale is None else value * scale
            return 0

        lax.fori_loop(0, count, body, 0, unroll=2)

    loads[2].wait()
    f0 = fields[0][0]
    unpack(own2d, f0, 0, rows)
    pl.semaphore_wait(barrier, nlon + nseg - 2)
    for copy in moves + static + halos[0][0]:
        copy.start()
    loads[3].wait()
    unpack(pat2d, press, 0, rows, STEP_SIZE)
    for copy in forcing:
        copy.start()

    def coefficients(first, count, group):
        def one(e, slot):
            at = lambda ref, k: ref[pl.ds((e + k) * blocks, blocks), :]
            w, w_e, w_w = at(wx, 0), at(wx, 1), at(wx, -1)
            u, u_w = at(ux, 0), at(ux, -1)
            up = pltpu.roll(w, 16, 1)
            down = pltpu.roll(w, 112, 1)
            up_wrap = jnp.where(sub8 == 0, 0.0, pltpu.roll(up, 1, 0))
            down_wrap = jnp.where(sub8 == 7, 0.0, pltpu.roll(down, 7, 0))
            south = jnp.where(lane8 < 16, up_wrap, up)
            north = jnp.where(lane8 >= 112, down_wrap, down)
            level = lane8 % DEPTH
            above = jnp.where(level == 0, 0.0, pltpu.roll(w, 1, 1))
            below = jnp.where(level == DEPTH - 1, 0.0, pltpu.roll(w, 127, 1))
            here = pl.ds(e * blocks, blocks)
            east_c[here, :] = w * (MIXING - jnp.minimum(u, 0.0))
            west_c[here, :] = w * (MIXING + jnp.maximum(u_w, 0.0))
            lat_c[here, :] = w * MIXING
            center = w * (
                1.0
                - MIXING * (w_e + w_w + north + south)
                - w_e * jnp.maximum(u, 0.0)
                + w_w * jnp.minimum(u_w, 0.0)
            )
            faces = w * (above + below)
            tot[2 * slot] = center
            tot[2 * slot + 1] = faces
            for b in range(blocks):
                a = tot[2 * slot, pl.ds(b, 8, stride=0), :]
                f = tot[2 * slot + 1, pl.ds(b, 8, stride=0), :]
                s = pl.ds(b * 128, 128)
                diag[e, :, s] = twice(a) - vmix * twice(f)
                vert[e, :, s] = vmix * row_w(e, b)

        def body(n, _):
            for slot in range(group):
                one(first + n * group + slot, slot)
            return 0

        lax.fori_loop(0, count // group, body, 0)

    def forces(first, count):
        def body(n, _):
            e = first + n
            for b in range(blocks):
                at = pl.ds(b * 128, 128)
                high, low = split(press[e, :, at])
                parts[e, 0:tracers, at] = high
                parts[e, tracers : 2 * tracers, at] = low
            return 0

        lax.fori_loop(0, count, body, 0, unroll=2 if count % 2 == 0 else count)

    def mix(src, s, es):
        cells = [[src[e, :, pl.ds(b * 128, 128)] for b in range(blocks)] for e in es]
        pairs = [split(c) for row in cells for c in row]
        dep = jnp.dot(
            jnp.concatenate([jnp.concatenate(hl, 1) for hl in pairs], 0),
            shift[...],
            preferred_element_type=F32,
        )
        results = []
        for n, e in enumerate(es):
            row = cells[n]
            mixed = []
            for q in range(blocks // 2):
                at = pl.ds(q * 256, 256)
                t = jnp.tanh(jnp.concatenate(row[2 * q : 2 * q + 2], 1)).astype(BF16)
                high, low = parts[e, 0:tracers, at], parts[e, tracers : 2 * tracers, at]
                mixed.append(
                    jnp.dot(
                        mixers[s], jnp.concatenate([t, t, high, high, low], 0), preferred_element_type=F32
                    )
                )
            first = n * blocks * tracers
            results.append(
                (row, [dep[first + b * tracers : first + (b + 1) * tracers] for b in range(blocks)], mixed)
            )
        return results

    def combine(src, dst, e, result, active):
        row, dep, mixed = result
        up = [pltpu.roll(c, 16, 1) for c in row]
        down = [pltpu.roll(c, 112, 1) for c in row]
        for b in range(blocks):
            at = pl.ds(b * 128, 128)
            spread = pl.ds(e * blocks + b, 8, stride=0)
            south = jnp.where(lane < 16, up[b - 1] if b else zero, up[b])
            north = jnp.where(lane >= 112, down[b + 1] if b < blocks - 1 else zero, down[b])
            fresh = diag[e, :, at] * row[b]
            fresh = fresh + twice(east_c[spread, :]) * src[e + 1, :, at]
            fresh = fresh + twice(west_c[spread, :]) * src[e - 1, :, at]
            fresh = fresh + twice(lat_c[spread, :]) * (south + north)
            fresh = fresh + vert[e, :, at] * dep[b]
            fresh = fresh + mixed[b // 2][:, b % 2 * 128 : b % 2 * 128 + 128]
            dst[e, :, at] = fresh if active is None else jnp.where(active, fresh, row[b])

    def update(s, level, es):
        src, dst = fields[s][level], fields[s][level + 1]
        active = alive(s, level) if level >= LEAST_STEPS else None
        waiting = None
        for i in range(0, len(es), UNROLL):
            group = es[i : i + UNROLL]
            results = mix(src, s, group)
            if waiting is not None:
                for e, result in zip(*waiting):
                    combine(src, dst, e, result, active)
            waiting = (group, results)
        for e, result in zip(*waiting):
            combine(src, dst, e, result, active)

    def span(s, level, first, count):
        def body(g, _):
            update(s, level, [first + g * (count // 2) + n for n in range(count // 2)])
            return 0

        lax.fori_loop(0, 2, body, 0)

    def alive(s, level):
        return jnp.full((tracers, 128), counts[own if s == 0 else prev], jnp.int32) > level

    def interior(s, base):
        for k in range(HALF):
            span(s, base + k, W + 1 + k, rows - 2 - 2 * k)

    def edges(s, base):
        for k in range(HALF):
            left, right = W - 2 + k, W + rows - 1 - k
            update(s, base + k, [left + n for n in range(3)] + [right + n for n in range(3)])

    def rim(s, base):
        for k in range(HALF):
            left, right = W - 2 + k, W + rows + 1 - k
            count = 7 - 2 * k
            update(s, base + k, [left + n for n in range(count)] + [right - n for n in range(count)])

    def middle(s, base):
        for k in range(HALF):
            span(s, base + k, W + 5 - k, rows - 10 + 2 * k)

    def residual(s, body_value):
        def body(r, acc):
            for b in range(blocks):
                at = pl.ds(b * 128, 128)
                value = fields[s][STEPS][r + W, :, at] - body_value(r, b)
                fields[s][STEPS][r + W, :, at] = value
                acc = acc + value * value
            return acc

        return lax.fori_loop(0, rows, body, zero, unroll=2)

    def publish(s, value):
        red[s, lon] = jnp.sum(jnp.where(first_diagonal, jnp.sum(value, axis=1, keepdims=True), 0.0), axis=0, keepdims=True)
        sends = []
        for p in range(1, nlon):
            peer = (lon + p) % nlon
            copy = remote(red.at[s, lon], red.at[s, lon], r_send.at[s, p], r_recv.at[s, p], (seg, peer))
            copy.start()
            sends.append(copy)
        return sends

    def finish(s, sends):
        for copy in sends:
            copy.wait()
        square = red[s, 0]
        for p in range(1, nlon):
            square = square + red[s, p]
        means = square / total_cells
        mean = jnp.broadcast_to(
            jnp.sum(jnp.where(first_diagonal, means, 0.0), axis=1, keepdims=True), (tracers, 128)
        )
        root = jnp.sqrt(mean + EPSILON)
        return means, root

    def scale(s, root, slot):
        inverse = 1.0 / root
        buffer = native.at[0] if s == 0 else near
        target = buffer.reshape(tracers * stride, 128)

        def body(r, _):
            for b in range(blocks):
                target[native_row(r, b), :] = fields[s][STEPS][r + W, :, pl.ds(b * 128, 128)] * inverse
            return 0

        lax.fori_loop(0, rows, body, 0, unroll=2)
        copy = pltpu.make_async_copy(buffer.at[:, pl.ds(0, native_rows)], out.at[slot], store_sem.at[s])
        copy.start()
        return copy

    coefficients(W + 1, rows - 2, 2)
    forces(W + 1, rows - 2)
    interior(0, 0)
    for copy in static:
        copy.wait()
    for copy in forcing:
        copy.wait()
    coefficients(1, W, W)
    coefficients(W + rows - 1, W, W)
    forces(1, W)
    forces(W + rows - 1, W)
    for copy in halos[0][0]:
        copy.wait()
    edges(0, 0)
    for copy in halos[0][1]:
        copy.start()

    g0 = fields[1][0]
    moves[0].wait()
    unpack(near2d, g0, 0, 8)
    halos[1][0][1].start()

    interior(0, HALF)
    moves[1].wait()
    unpack(near2d, g0, rows - 8, 8)
    halos[1][0][0].start()
    for copy in halos[0][1]:
        copy.wait()
    edges(0, HALF)
    loads[4].wait()
    sends_own = publish(0, residual(0, lambda r, b: own2d_1[native_row(r, b), :] * row_w(r + W, b)))

    for copy in moves[2:]:
        copy.wait()
    unpack(near2d, g0, 8, rows - 16)
    for copy in halos[1][0]:
        copy.wait()
    rim(1, 0)
    for copy in halos[1][1]:
        copy.start()
    middle(1, 0)
    interior(1, HALF)
    for copy in halos[1][1]:
        copy.wait()
    edges(1, HALF)
    sends_prev = publish(1, residual(1, lambda r, b: fields[0][0][r + W, :, pl.ds(b * 128, 128)]))
    mean_own, root_own = finish(0, sends_own)
    stored = [scale(0, root_own, 1)]
    mean_prev, root_prev = finish(1, sends_prev)

    local = jnp.where(lane[0:1] < tracers, mean_own + mean_prev, 0.0)
    year[seg] = jnp.broadcast_to(jnp.sum(local, axis=1, keepdims=True), (1, 128))
    sends = []
    for p in range(1, nseg):
        peer = (seg + p) % nseg
        copy = remote(year.at[seg], year.at[seg], y_send.at[p], y_recv.at[p], (peer, lon))
        copy.start()
        sends.append(copy)
    stored.append(scale(1, root_prev, 0))
    for copy in sends:
        copy.wait()
    total = year[0]
    for p in range(1, nseg):
        total = total + year[p]
    for copy in stored:
        copy.wait()
    mismatch[0, 0] = jnp.sqrt(total / (2 * nseg * tracers))[0, 0]


def shards(mesh, states, step_counts, land, east_flow, vert_mix, coupling, amplitude, pattern):
    nseg, nlon = mesh.shape["seg"], mesh.shape["lon"]
    per, tracers, rows, cols = states.shape
    blocks = cols // 128
    stride = rows * blocks

    def tiles(x):
        lead = x.shape[:-2]
        x = x.reshape(lead + (rows // 8, 8, blocks, 128))
        return jnp.swapaxes(x, -2, -3).reshape(lead + (stride, 128))

    ext = rows + 2 * HALF
    any_spec = pl.BlockSpec(memory_space=pl.ANY)
    smem = pl.BlockSpec(memory_space=pltpu.SMEM)
    vmem = pl.BlockSpec(memory_space=pltpu.VMEM)
    dma = pltpu.SemaphoreType.DMA
    dims = (nseg, nlon, tracers, rows, cols, rows * nlon * cols)
    out, mismatch = pl.pallas_call(
        functools.partial(kernel, dims),
        out_shape=(
            jax.ShapeDtypeStruct((per, tracers, stride, 128), F32),
            jax.ShapeDtypeStruct((1, 1), F32),
        ),
        in_specs=[any_spec] * 4 + [smem] * 3 + [vmem],
        out_specs=(any_spec, smem),
        scratch_shapes=[
            *[pltpu.VMEM((ext, tracers, cols), F32)] * 10,
            *[pltpu.VMEM((ext, tracers, cols), F32)] * 3,
            pltpu.VMEM((ext, 2 * tracers, cols), BF16),
            pltpu.VMEM((ext * blocks, 128), F32),
            pltpu.VMEM((ext * blocks, 128), F32),
            pltpu.VMEM((ext * blocks, 128), F32),
            pltpu.VMEM((ext * blocks, 128), F32),
            pltpu.VMEM((ext * blocks, 128), F32),
            pltpu.VMEM((tracers, stride + 8, 128), F32),
            pltpu.VMEM((2, tracers, stride + 8, 128), F32),
            pltpu.VMEM((tracers, stride + 8, 128), F32),
            pltpu.VMEM((stride, 128), jnp.int32),
            pltpu.VMEM((stride, 128), F32),
            pltpu.VMEM((256, 128), BF16),
            pltpu.VMEM((2, nlon, 1, 128), F32),
            pltpu.VMEM((nseg, 1, 128), F32),
            pltpu.VMEM((2 * HALF, 8, 128), F32),
            pltpu.VMEM((tracers, 128), F32),
            dma((5,)),
            dma((2,)),
            dma((rows // 8,)),
            dma((rows // 8,)),
            dma((2, 2, 2)),
            dma((2, 2, 2)),
            dma((3, 2)),
            dma((3, 2)),
            dma((2, nlon)),
            dma((2, nlon)),
            dma((nseg,)),
            dma((nseg,)),
        ],
        compiler_params=pltpu.CompilerParams(
            collective_id=0, has_side_effects=True, vmem_limit_bytes=44 * 1024 * 1024
        ),
    )(
        *(
            pltpu.with_memory_space_constraint(x, pltpu.HBM)
            for x in (
                tiles(states),
                tiles(pattern),
                tiles(land),
                tiles(east_flow),
                step_counts,
                vert_mix,
                amplitude.T,
                coupling,
            )
        )
    )
    out = out.reshape(per, tracers, rows // 8, blocks, 8, 128)
    out = jnp.swapaxes(out, -2, -3).reshape(states.shape)
    return out, mismatch.reshape(())


def solution(mesh):
    in_specs = (
        P("seg", None, "lon", None),
        P(),
        P("lon", None),
        P("lon", None),
        P(),
        P(),
        P(),
        P(None, "lon", None),
    )
    out_specs = (P("seg", None, "lon", None), P())
    return jax.shard_map(
        functools.partial(shards, mesh), mesh=mesh, in_specs=in_specs, out_specs=out_specs, check_vma=False
    )
```

```python
import functools

import jax
import jax.numpy as jnp
from jax import lax
from jax.experimental import pallas as pl
from jax.experimental.pallas import tpu as pltpu
from jax.sharding import PartitionSpec as P

STEPS = 6
DEPTH = 16
MIXING = 0.1
STEP_SIZE = 0.1
EPSILON = 1e-06

HALF = 3
UNROLL = 4
LEAST_STEPS = 4
MESH = pl.DeviceIdType.MESH
F32 = jnp.float32
BF16 = jnp.bfloat16


def split(x):
    high = x.astype(BF16)
    return high, (x - high.astype(F32)).astype(BF16)


def twice(x):
    return jnp.concatenate([x, x], 0)


def column(values, tracers):
    row = lax.broadcasted_iota(jnp.int32, (tracers, 128), 0)
    out = jnp.zeros((tracers, 128), F32)
    for t in range(tracers):
        out = jnp.where(row == t, values(t), out)
    return out


def kernel(
    dims,
    states,
    pattern,
    land,
    flow,
    counts,
    vert_mix,
    amplitude,
    coupling,
    out,
    mismatch,
    f_own_0,
    f_own_3,
    f_own_6,
    f_prev_0,
    f_prev_3,
    f_prev_6,
    f_1,
    f_2,
    f_4,
    f_5,
    diag,
    vert,
    press,
    parts,
    wx,
    ux,
    east_c,
    west_c,
    lat_c,
    near,
    native,
    native_p,
    native_land,
    native_flow,
    shift,
    red,
    year,
    tot,
    lhs,
    load_sem,
    store_sem,
    z_send,
    z_recv,
    h_send,
    h_recv,
    s_send,
    s_recv,
    r_send,
    r_recv,
    y_send,
    y_recv,
):
    nseg, nlon, tracers, rows, cols, total_cells = dims
    blocks = cols // 128
    band = 8 * blocks
    native_rows = rows // 8 * band
    stride = native_rows + 8
    fields = ((f_own_0, f_1, f_2, f_own_3, f_4, f_5, f_own_6), (f_prev_0, f_1, f_2, f_prev_3, f_4, f_5, f_prev_6))
    seg = lax.axis_index("seg")
    lon = lax.axis_index("lon")
    lane = lax.broadcasted_iota(jnp.int32, (tracers, 128), 1)
    lane8 = lax.broadcasted_iota(jnp.int32, (8, 128), 1)
    sub8 = lax.broadcasted_iota(jnp.int32, (8, 128), 0)
    zero = jnp.zeros((tracers, 128), F32)
    W = HALF

    barrier = pltpu.get_barrier_semaphore()
    for p in range(1, nlon):
        pl.semaphore_signal(barrier, inc=1, device_id=(seg, (lon + p) % nlon), device_id_type=MESH)
    for p in range(1, nseg):
        pl.semaphore_signal(barrier, inc=1, device_id=((seg + p) % nseg, lon), device_id_type=MESH)

    loads = [
        pltpu.make_async_copy(land, native_land, load_sem.at[0]),
        pltpu.make_async_copy(flow, native_flow, load_sem.at[1]),
        pltpu.make_async_copy(states.at[0], native.at[0, :, pl.ds(0, native_rows)], load_sem.at[2]),
        pltpu.make_async_copy(pattern, native_p.at[:, pl.ds(0, native_rows)], load_sem.at[3]),
        pltpu.make_async_copy(states.at[1], native.at[1, :, pl.ds(0, native_rows)], load_sem.at[4]),
    ]
    for copy in loads[:4]:
        copy.start()

    loads[0].wait()
    loads[1].wait()
    for r in range(rows):
        start = r // 8 * band + r % 8
        wx[pl.ds((r + W) * blocks, blocks), :] = native_land[
            pl.ds(start, blocks, stride=8), :
        ].astype(F32)
        ux[pl.ds((r + W) * blocks, blocks), :] = native_flow[pl.ds(start, blocks, stride=8), :]

    east = (seg, (lon + 1) % nlon)
    west = (seg, (lon + nlon - 1) % nlon)

    def remote(src, dst, send, recv, device):
        return pltpu.make_async_remote_copy(
            src_ref=src, dst_ref=dst, send_sem=send, recv_sem=recv, device_id=device, device_id_type=MESH
        )

    def halo(ref, width, send, recv, scale=1):
        return [
            remote(
                ref.at[pl.ds((W + rows - width) * scale, width * scale)],
                ref.at[pl.ds((W - width) * scale, width * scale)],
                send.at[0],
                recv.at[0],
                east,
            ),
            remote(
                ref.at[pl.ds(W * scale, width * scale)],
                ref.at[pl.ds((W + rows) * scale, width * scale)],
                send.at[1],
                recv.at[1],
                west,
            ),
        ]

    nxt = ((seg + 1) % nseg, lon)
    chunks = (0, rows // 8 - 1) + tuple(range(1, rows // 8 - 1))
    moves = [
        remote(
            states.at[1, :, pl.ds(b * band, band), :],
            near.at[:, pl.ds(b * band, band), :],
            z_send.at[n],
            z_recv.at[n],
            nxt,
        )
        for n, b in enumerate(chunks)
    ]
    static = (
        halo(wx, W, s_send.at[0], s_recv.at[0], blocks)
        + halo(ux, W, s_send.at[1], s_recv.at[1], blocks)
    )
    forcing = halo(press, W - 1, s_send.at[2], s_recv.at[2])
    halos = [
        [halo(fields[s][level], W, h_send.at[s, n], h_recv.at[s, n]) for n, level in enumerate((0, HALF))]
        for s in (0, 1)
    ]

    def row_w(e, b):
        return twice(wx[pl.ds(e * blocks + b, 8, stride=0), :])

    def native_row(r, b):
        return pl.ds(r // 8 * band + b * 8 + r % 8, tracers, stride=stride)

    own2d = native.at[0].reshape(tracers * stride, 128)
    own2d_1 = native.at[1].reshape(tracers * stride, 128)
    near2d = near.reshape(tracers * stride, 128)
    pat2d = native_p.reshape(tracers * stride, 128)

    def unpack(src2d, dst, first, count, scale=None):
        def body(n, _):
            r = first + n
            for b in range(blocks):
                value = src2d[native_row(r, b), :] * row_w(r + W, b)
                dst[r + W, :, pl.ds(b * 128, 128)] = value if scale is None else value * scale
            return 0

        lax.fori_loop(0, count, body, 0, unroll=2)

    loads[2].wait()
    f0 = fields[0][0]
    unpack(own2d, f0, 0, rows)
    pl.semaphore_wait(barrier, nlon + nseg - 2)
    for copy in moves + static + halos[0][0]:
        copy.start()
    loads[4].start()

    i = lax.broadcasted_iota(jnp.int32, (256, 128), 0) % 128
    j = lax.broadcasted_iota(jnp.int32, (256, 128), 1)
    apart = (i - j) * (i - j) == 1
    shift[...] = jnp.where(apart & (i // DEPTH == j // DEPTH), 1.0, 0.0).astype(BF16)
    own = 2 * seg
    prev = (own + 2 * nseg - 1) % (2 * nseg)
    vmix = column(lambda t: vert_mix[t], tracers)

    lhs[...] = jnp.zeros((tracers, 128), F32)
    lhs[:, 0:tracers] = coupling[...] * STEP_SIZE
    c_high, c_low = (x.astype(F32) for x in split(lhs[...]))
    c_low = pltpu.roll(c_low, tracers, 1)
    place = lane // tracers
    on_diagonal = lane % tracers == lax.broadcasted_iota(jnp.int32, (tracers, 128), 0)
    first_diagonal = on_diagonal & (place == 0)
    mixers = []
    for s in (own, prev):
        a_high, a_low = (
            jnp.where(on_diagonal, x.astype(F32), 0.0)
            for x in split(column(lambda t, s=s: amplitude[t, s], tracers))
        )
        joined = jnp.where(place == 0, c_high, jnp.where(place == 1, c_low, jnp.where(place == 3, a_low, a_high)))
        mixers.append(joined.astype(BF16)[:, : 5 * tracers])

    loads[3].wait()
    unpack(pat2d, press, 0, rows, STEP_SIZE)
    for copy in forcing:
        copy.start()

    def coefficients(first, count, group):
        def one(e, slot):
            at = lambda ref, k: ref[pl.ds((e + k) * blocks, blocks), :]
            w, w_e, w_w = at(wx, 0), at(wx, 1), at(wx, -1)
            u, u_w = at(ux, 0), at(ux, -1)
            up = pltpu.roll(w, 16, 1)
            down = pltpu.roll(w, 112, 1)
            up_wrap = jnp.where(sub8 == 0, 0.0, pltpu.roll(up, 1, 0))
            down_wrap = jnp.where(sub8 == 7, 0.0, pltpu.roll(down, 7, 0))
            south = jnp.where(lane8 < 16, up_wrap, up)
            north = jnp.where(lane8 >= 112, down_wrap, down)
            level = lane8 % DEPTH
            above = jnp.where(level == 0, 0.0, pltpu.roll(w, 1, 1))
            below = jnp.where(level == DEPTH - 1, 0.0, pltpu.roll(w, 127, 1))
            here = pl.ds(e * blocks, blocks)
            east_c[here, :] = w * (MIXING - jnp.minimum(u, 0.0))
            west_c[here, :] = w * (MIXING + jnp.maximum(u_w, 0.0))
            lat_c[here, :] = w * MIXING
            center = w * (
                1.0
                - MIXING * (w_e + w_w + north + south)
                - w_e * jnp.maximum(u, 0.0)
                + w_w * jnp.minimum(u_w, 0.0)
            )
            faces = w * (above + below)
            tot[2 * slot] = center
            tot[2 * slot + 1] = faces
            for b in range(blocks):
                a = tot[2 * slot, pl.ds(b, 8, stride=0), :]
                f = tot[2 * slot + 1, pl.ds(b, 8, stride=0), :]
                s = pl.ds(b * 128, 128)
                diag[e, :, s] = twice(a) - vmix * twice(f)
                vert[e, :, s] = vmix * row_w(e, b)

        def body(n, _):
            for slot in range(group):
                one(first + n * group + slot, slot)
            return 0

        lax.fori_loop(0, count // group, body, 0)

    def forces(first, count):
        def body(n, _):
            e = first + n
            for b in range(blocks):
                at = pl.ds(b * 128, 128)
                high, low = split(press[e, :, at])
                parts[e, 0:tracers, at] = high
                parts[e, tracers : 2 * tracers, at] = low
            return 0

        lax.fori_loop(0, count, body, 0, unroll=2 if count % 2 == 0 else count)

    def mix(src, s, es):
        cells = [[src[e, :, pl.ds(b * 128, 128)] for b in range(blocks)] for e in es]
        pairs = [split(c) for row in cells for c in row]
        dep = jnp.dot(
            jnp.concatenate([jnp.concatenate(hl, 1) for hl in pairs], 0),
            shift[...],
            preferred_element_type=F32,
        )
        results = []
        for n, e in enumerate(es):
            row = cells[n]
            mixed = []
            for q in range(blocks // 2):
                at = pl.ds(q * 256, 256)
                t = jnp.tanh(jnp.concatenate(row[2 * q : 2 * q + 2], 1)).astype(BF16)
                high, low = parts[e, 0:tracers, at], parts[e, tracers : 2 * tracers, at]
                mixed.append(
                    jnp.dot(
                        mixers[s], jnp.concatenate([t, t, high, high, low], 0), preferred_element_type=F32
                    )
                )
            first = n * blocks * tracers
            results.append(
                (row, [dep[first + b * tracers : first + (b + 1) * tracers] for b in range(blocks)], mixed)
            )
        return results

    def combine(src, dst, e, result, active):
        row, dep, mixed = result
        up = [pltpu.roll(c, 16, 1) for c in row]
        down = [pltpu.roll(c, 112, 1) for c in row]
        for b in range(blocks):
            at = pl.ds(b * 128, 128)
            spread = pl.ds(e * blocks + b, 8, stride=0)
            south = jnp.where(lane < 16, up[b - 1] if b else zero, up[b])
            north = jnp.where(lane >= 112, down[b + 1] if b < blocks - 1 else zero, down[b])
            fresh = diag[e, :, at] * row[b]
            fresh = fresh + twice(east_c[spread, :]) * src[e + 1, :, at]
            fresh = fresh + twice(west_c[spread, :]) * src[e - 1, :, at]
            fresh = fresh + twice(lat_c[spread, :]) * (south + north)
            fresh = fresh + vert[e, :, at] * dep[b]
            fresh = fresh + mixed[b // 2][:, b % 2 * 128 : b % 2 * 128 + 128]
            dst[e, :, at] = fresh if active is None else jnp.where(active, fresh, row[b])

    def update(s, level, es):
        src, dst = fields[s][level], fields[s][level + 1]
        active = alive(s, level) if level >= LEAST_STEPS else None
        waiting = None
        for i in range(0, len(es), UNROLL):
            group = es[i : i + UNROLL]
            results = mix(src, s, group)
            if waiting is not None:
                for e, result in zip(*waiting):
                    combine(src, dst, e, result, active)
            waiting = (group, results)
        for e, result in zip(*waiting):
            combine(src, dst, e, result, active)

    def span(s, level, first, count):
        def body(g, _):
            update(s, level, [first + g * (count // 2) + n for n in range(count // 2)])
            return 0

        lax.fori_loop(0, 2, body, 0)

    def alive(s, level):
        return jnp.full((tracers, 128), counts[own if s == 0 else prev], jnp.int32) > level

    def interior(s, base):
        for k in range(HALF):
            span(s, base + k, W + 1 + k, rows - 2 - 2 * k)

    def edges(s, base):
        for k in range(HALF):
            left, right = W - 2 + k, W + rows - 1 - k
            update(s, base + k, [left + n for n in range(3)] + [right + n for n in range(3)])

    def rim(s, base):
        for k in range(HALF):
            left, right = W - 2 + k, W + rows + 1 - k
            count = 7 - 2 * k
            update(s, base + k, [left + n for n in range(count)] + [right - n for n in range(count)])

    def core(s, base):
        span(s, base, W + 5, rows - 10)
        span(s, base + 1, W + 6, rows - 12)

    def middle(s, base):
        last = W + rows - 1
        update(s, base + 1, [W + 4, W + 5, last - 5, last - 4])
        span(s, base + 2, W + 3, rows - 6)

    def residual(s, body_value):
        def body(r, acc):
            for b in range(blocks):
                at = pl.ds(b * 128, 128)
                value = fields[s][STEPS][r + W, :, at] - body_value(r, b)
                fields[s][STEPS][r + W, :, at] = value
                acc = acc + value * value
            return acc

        return lax.fori_loop(0, rows, body, zero, unroll=2)

    def publish(s, value):
        red[s, lon] = jnp.sum(jnp.where(first_diagonal, jnp.sum(value, axis=1, keepdims=True), 0.0), axis=0, keepdims=True)
        sends = []
        for p in range(1, nlon):
            peer = (lon + p) % nlon
            copy = remote(red.at[s, lon], red.at[s, lon], r_send.at[s, p], r_recv.at[s, p], (seg, peer))
            copy.start()
            sends.append(copy)
        return sends

    def finish(s, sends):
        for copy in sends:
            copy.wait()
        square = red[s, 0]
        for p in range(1, nlon):
            square = square + red[s, p]
        means = square / total_cells
        mean = jnp.broadcast_to(
            jnp.sum(jnp.where(first_diagonal, means, 0.0), axis=1, keepdims=True), (tracers, 128)
        )
        root = jnp.sqrt(mean + EPSILON)
        return means, root

    def scale(s, root, slot):
        inverse = 1.0 / root
        buffer = native.at[0] if s == 0 else near
        target = buffer.reshape(tracers * stride, 128)

        def body(r, _):
            for b in range(blocks):
                target[native_row(r, b), :] = fields[s][STEPS][r + W, :, pl.ds(b * 128, 128)] * inverse
            return 0

        lax.fori_loop(0, rows, body, 0, unroll=2)
        copy = pltpu.make_async_copy(buffer.at[:, pl.ds(0, native_rows)], out.at[slot], store_sem.at[s])
        copy.start()
        return copy

    coefficients(W + 1, rows - 2, 2)
    forces(W + 1, rows - 2)
    interior(0, 0)
    for copy in static:
        copy.wait()
    for copy in forcing:
        copy.wait()
    coefficients(1, W, W)
    coefficients(W + rows - 1, W, W)
    forces(1, W)
    forces(W + rows - 1, W)
    for copy in halos[0][0]:
        copy.wait()
    edges(0, 0)
    for copy in halos[0][1]:
        copy.start()

    g0 = fields[1][0]
    moves[0].wait()
    unpack(near2d, g0, 0, 8)
    halos[1][0][1].start()

    interior(0, HALF)
    moves[1].wait()
    unpack(near2d, g0, rows - 8, 8)
    halos[1][0][0].start()
    for copy in halos[0][1]:
        copy.wait()
    edges(0, HALF)

    for copy in moves[2:]:
        copy.wait()
    unpack(near2d, g0, 8, rows - 16)
    core(1, 0)
    for copy in halos[1][0]:
        copy.wait()
    rim(1, 0)
    for copy in halos[1][1]:
        copy.start()
    loads[4].wait()
    sends_own = publish(0, residual(0, lambda r, b: own2d_1[native_row(r, b), :] * row_w(r + W, b)))
    middle(1, 0)
    interior(1, HALF)
    for copy in halos[1][1]:
        copy.wait()
    edges(1, HALF)
    sends_prev = publish(1, residual(1, lambda r, b: fields[0][0][r + W, :, pl.ds(b * 128, 128)]))
    mean_own, root_own = finish(0, sends_own)
    stored = [scale(0, root_own, 1)]
    mean_prev, root_prev = finish(1, sends_prev)

    local = jnp.where(lane[0:1] < tracers, mean_own + mean_prev, 0.0)
    year[seg] = jnp.broadcast_to(jnp.sum(local, axis=1, keepdims=True), (1, 128))
    sends = []
    for p in range(1, nseg):
        peer = (seg + p) % nseg
        copy = remote(year.at[seg], year.at[seg], y_send.at[p], y_recv.at[p], (peer, lon))
        copy.start()
        sends.append(copy)
    stored.append(scale(1, root_prev, 0))
    for copy in sends:
        copy.wait()
    total = year[0]
    for p in range(1, nseg):
        total = total + year[p]
    for copy in stored:
        copy.wait()
    mismatch[0, 0] = jnp.sqrt(total / (2 * nseg * tracers))[0, 0]


def shards(mesh, states, step_counts, land, east_flow, vert_mix, coupling, amplitude, pattern):
    nseg, nlon = mesh.shape["seg"], mesh.shape["lon"]
    per, tracers, rows, cols = states.shape
    blocks = cols // 128
    stride = rows * blocks

    def tiles(x):
        lead = x.shape[:-2]
        x = x.reshape(lead + (rows // 8, 8, blocks, 128))
        return jnp.swapaxes(x, -2, -3).reshape(lead + (stride, 128))

    ext = rows + 2 * HALF
    any_spec = pl.BlockSpec(memory_space=pl.ANY)
    smem = pl.BlockSpec(memory_space=pltpu.SMEM)
    vmem = pl.BlockSpec(memory_space=pltpu.VMEM)
    dma = pltpu.SemaphoreType.DMA
    dims = (nseg, nlon, tracers, rows, cols, rows * nlon * cols)
    out, mismatch = pl.pallas_call(
        functools.partial(kernel, dims),
        out_shape=(
            jax.ShapeDtypeStruct((per, tracers, stride, 128), F32),
            jax.ShapeDtypeStruct((1, 1), F32),
        ),
        in_specs=[any_spec] * 4 + [smem] * 3 + [vmem],
        out_specs=(any_spec, smem),
        scratch_shapes=[
            *[pltpu.VMEM((ext, tracers, cols), F32)] * 10,
            *[pltpu.VMEM((ext, tracers, cols), F32)] * 3,
            pltpu.VMEM((ext, 2 * tracers, cols), BF16),
            pltpu.VMEM((ext * blocks, 128), F32),
            pltpu.VMEM((ext * blocks, 128), F32),
            pltpu.VMEM((ext * blocks, 128), F32),
            pltpu.VMEM((ext * blocks, 128), F32),
            pltpu.VMEM((ext * blocks, 128), F32),
            pltpu.VMEM((tracers, stride + 8, 128), F32),
            pltpu.VMEM((2, tracers, stride + 8, 128), F32),
            pltpu.VMEM((tracers, stride + 8, 128), F32),
            pltpu.VMEM((stride, 128), jnp.int32),
            pltpu.VMEM((stride, 128), F32),
            pltpu.VMEM((256, 128), BF16),
            pltpu.VMEM((2, nlon, 1, 128), F32),
            pltpu.VMEM((nseg, 1, 128), F32),
            pltpu.VMEM((2 * HALF, 8, 128), F32),
            pltpu.VMEM((tracers, 128), F32),
            dma((5,)),
            dma((2,)),
            dma((rows // 8,)),
            dma((rows // 8,)),
            dma((2, 2, 2)),
            dma((2, 2, 2)),
            dma((3, 2)),
            dma((3, 2)),
            dma((2, nlon)),
            dma((2, nlon)),
            dma((nseg,)),
            dma((nseg,)),
        ],
        compiler_params=pltpu.CompilerParams(
            collective_id=0, has_side_effects=True, vmem_limit_bytes=44 * 1024 * 1024
        ),
    )(
        *(
            pltpu.with_memory_space_constraint(x, pltpu.HBM)
            for x in (
                tiles(states),
                tiles(pattern),
                tiles(land),
                tiles(east_flow),
                step_counts,
                vert_mix,
                amplitude.T,
                coupling,
            )
        )
    )
    out = out.reshape(per, tracers, rows // 8, blocks, 8, 128)
    out = jnp.swapaxes(out, -2, -3).reshape(states.shape)
    return out, mismatch.reshape(())


def solution(mesh):
    in_specs = (
        P("seg", None, "lon", None),
        P(),
        P("lon", None),
        P("lon", None),
        P(),
        P(),
        P(),
        P(None, "lon", None),
    )
    out_specs = (P("seg", None, "lon", None), P())
    return jax.shard_map(
        functools.partial(shards, mesh), mesh=mesh, in_specs=in_specs, out_specs=out_specs, check_vma=False
    )
```
